32 devices in a mesh: dp: 8 (over y, x, core), seq: 4 (over z).
Axes of the slice: x: 2, y: 2, z: 4, core: 2. Of those that a mesh axis runs over, the one named last changes fastest.
Arguments:
- queries: bfloat16 [8, 4, 512, 32, 128], P('dp', 'seq'), may hold values from -6 to 6
- key_rows: bfloat16 [8, 4, 512, 32, 128], P('dp', 'seq'), may hold values from -6 to 6
- value_rows: bfloat16 [8, 4, 512, 32, 128], P('dp', 'seq'), may hold values from -6 to 6
- destination: int32 [8, 4, 512], P('dp', 'seq'), may hold values from 0 to 7, as said below
- doc_starts: int32 [8, 4, 512], P('dp', 'seq'), may hold values 0 or 1
- decay_rate: float32 [32], replicated, may hold values from 7.6293945e-06 to 0.04
- norm_gain: float32 [32, 128], replicated, may hold values from 0.1 to 1.9
Outputs:
- attended: bfloat16 [8, 4, 512, 32, 128], P('dp', 'seq')
The draws below stay inside these ranges and needn't reach their ends.
Inputs may be any that keep to these rules, and one draw needn't show every extreme that they name: `destination`: each loader sends at most 96 of its rows to one sequence; at each seq index one sequence, drawn afresh, receives exactly 96 rows from every loader.
All inputs are finite; a program needn't handle non-finite values. No bound on the sum of `doc_starts` on one device may be relied on, other than what follows from the above.
Results may differ from the reference program's by a relative error of at most 0.0055.
Values may be sent and summed in bfloat16 or wider, within the bound.
A program may use at most 192 MiB of HBM per device.

```python
import math
import jax
import jax.numpy as jnp
from jax import lax

H = 32
DH = 128
BLK = 384
TOK_DEV = 512
LOADERS = 8
SHARDS = 4
CAP = 96
CHAIN = 2048


def draw_destination(key, part):
    hot_key, row_key = jax.random.split(jax.random.fold_in(key, 11))
    hot_seq = jax.random.randint(hot_key, (SHARDS,), 0, LOADERS).astype(jnp.int32)
    hot_all = jnp.tile(hot_seq, LOADERS)
    row_keys = jax.random.split(row_key, LOADERS * SHARDS)

    def one_loader(loader_key, hot_target):
        pick_key, order_key = jax.random.split(loader_key)
        picks = jax.random.permutation(pick_key, (LOADERS - 1) * CAP)[:TOK_DEV - CAP].astype(jnp.int32)
        others = picks // CAP
        others = others + (others >= hot_target).astype(jnp.int32)
        targets = jnp.concatenate([jnp.full((CAP,), hot_target, jnp.int32), others.astype(jnp.int32)])
        order = jax.random.permutation(order_key, TOK_DEV).astype(jnp.int32)
        return targets[order]
    rows = jax.vmap(one_loader)(row_keys, hot_all)
    return rows.reshape(LOADERS, SHARDS, TOK_DEV).astype(jnp.int32)


def draw_decay_rate(key, part):
    uniform_part = jax.random.uniform(jax.random.fold_in(key, 23), (H,), jnp.float32)
    low_end = math.log(1.0 / (64.0 * CHAIN))
    high_end = math.log(1.0 / 25.0)
    return jnp.exp(low_end + (high_end - low_end) * uniform_part).astype(jnp.float32)


def touch_ends(result, rng, least, top_value):
    longest = result.shape.index(max(result.shape))
    spots = []
    for shift in (0, 1):
        where = [jax.random.randint(jax.random.fold_in(rng, axis), (), 0, length) for axis, length in enumerate(result.shape)]
        where[longest] = (where[longest] + shift) % result.shape[longest]
        spots.append(tuple(where))
    return result.at[spots[0]].set(least).at[spots[1]].set(top_value)


def level_of(rng, shape, cuts, smallest, high):
    level, own = 1.0, jax.random.fold_in(rng, 6)
    for dim, blocks in cuts:
        heights = jnp.exp(jax.random.uniform(jax.random.fold_in(own, dim), (blocks,), jnp.float32, smallest / len(cuts), high / len(cuts)))
        level = level * jnp.repeat(heights, shape[dim] // blocks).reshape([-1 if axis == dim else 1 for axis in range(len(shape))])
    return level


def gaussian(rng, shape, spread, reach, cuts=(), held_as=jnp.bfloat16):
    factor_of = level_of(rng, shape, cuts, -0.22, 0.18) if cuts else 1.0
    array = jax.random.normal(rng, shape, jnp.float32) * spread * factor_of
    return jnp.minimum(jnp.maximum(array, -reach), reach).astype(held_as)


def setup_inputs(seed: int = 0) -> dict:
    streams_of = jax.random.split(jax.random.key(seed), 8)
    return {
        "queries": gaussian(streams_of[0], (LOADERS, SHARDS, TOK_DEV, H, DH), 1.0, 6.0, ((0, 8), (1, 4))),
        "key_rows": gaussian(streams_of[1], (LOADERS, SHARDS, TOK_DEV, H, DH), 1.0, 6.0, ((0, 8), (1, 4))),
        "value_rows": gaussian(streams_of[2], (LOADERS, SHARDS, TOK_DEV, H, DH), 1.0, 6.0, ((0, 8), (1, 4))),
        "destination": draw_destination(jax.random.fold_in(streams_of[7], 71), 0),
        "doc_starts": touch_ends((jax.random.randint(streams_of[4], (LOADERS, SHARDS, TOK_DEV), 0, 4 * CHAIN) < 1).astype(jnp.int32), jax.random.fold_in(streams_of[4], 1), 0, 1),
        "decay_rate": draw_decay_rate(jax.random.fold_in(streams_of[7], 71), 0),
        "norm_gain": jnp.clip(1.0 + 0.18 * jax.random.normal(streams_of[6], (H, DH), jnp.float32), 0.1, 1.9),
    }


eps_norm = 1e-06

def to_half(values_in):
    return lax.optimization_barrier(values_in.astype(jnp.bfloat16)).astype(jnp.float32)

def attend_block(carry_state, block_inputs, decay_rate, norm_gain):
    block_query, block_key, block_value, block_count, block_doc, block_live, block_start = block_inputs
    before_count = block_count[0] - block_live[0]
    before_doc = block_doc[0] - block_start[0]
    positions = jnp.arange(BLK, dtype=jnp.int32)
    causal = positions[:, None] >= positions[None, :]
    same_doc = block_doc[:, None] == block_doc[None, :]
    keep_mask = causal & same_doc & (block_live[None, :] == 1)
    distance = jnp.maximum(block_count[:, None] - block_count[None, :], 0).astype(jnp.float32)
    weight = jnp.where(keep_mask[None], jnp.exp(-decay_rate[:, None, None] * distance[None]), 0.0)
    query_wide = block_query.astype(jnp.float32)
    key_wide = block_key.astype(jnp.float32)
    value_wide = block_value.astype(jnp.float32)
    scores = jnp.einsum('phd,qhd->hpq', query_wide, key_wide)
    weights_half = to_half(scores * weight)
    intra_term = jnp.einsum('hpq,qhd->phd', weights_half, value_wide)
    since = (block_count - before_count).astype(jnp.float32)
    carry_weight = jnp.where((block_doc == before_doc)[:, None], jnp.exp(-decay_rate[None, :] * since[:, None]), 0.0)
    state_half = to_half(carry_state)
    inter_term = jnp.einsum('phd,hde->phe', query_wide, state_half) * carry_weight[:, :, None]
    mixed_out = intra_term + inter_term
    end_count = block_count[-1]
    end_doc = block_doc[-1]
    until = (end_count - block_count).astype(jnp.float32)
    key_keep = (block_live == 1) & (block_doc == end_doc)
    key_weight = jnp.where(key_keep[:, None], jnp.exp(-decay_rate[None, :] * until[:, None]), 0.0)
    scaled_keys = to_half(key_wide * key_weight[:, :, None])
    update = jnp.einsum('phd,phe->hde', scaled_keys, value_wide)
    block_span = (end_count - before_count).astype(jnp.float32)
    block_decay = jnp.where(end_doc == before_doc, jnp.exp(-decay_rate * block_span), 0.0)
    new_state = block_decay[:, None, None] * carry_state + update
    mean_square = lax.optimization_barrier(jnp.mean(mixed_out * mixed_out, axis=(1, 2)))
    normed = (mixed_out * lax.rsqrt(mean_square + eps_norm)[:, None, None] * norm_gain[None]).astype(jnp.bfloat16)
    return (new_state, normed)

def attend_sequence(table_query, table_key, table_value, table_live, table_start, decay_rate, norm_gain):
    total = SHARDS * LOADERS * CAP
    live_flat = table_live.reshape(total)
    start_flat = table_start.reshape(total)
    live_count = jnp.cumsum(live_flat, dtype=jnp.int32)
    doc_count = jnp.cumsum(start_flat, dtype=jnp.int32)
    block_total = total // BLK

    def shaped(values_in):
        return values_in.reshape((block_total, BLK) + values_in.shape[3:])
    block_inputs = (shaped(table_query), shaped(table_key), shaped(table_value), live_count.reshape(block_total, BLK), doc_count.reshape(block_total, BLK), live_flat.reshape(block_total, BLK), start_flat.reshape(block_total, BLK))

    def advance(carry_state, inputs):
        return attend_block(carry_state, inputs, decay_rate, norm_gain)
    first_state = jnp.zeros((H, DH, DH), jnp.float32)
    final_state, normed = lax.scan(advance, first_state, block_inputs)
    return normed.reshape(SHARDS, LOADERS, CAP, H, DH)

def reference(queries, key_rows, value_rows, destination, doc_starts, decay_rate, norm_gain):
    targets = jnp.arange(LOADERS, dtype=jnp.int32)
    onehot = (destination[..., None] == targets).astype(jnp.int32)
    slot = lax.optimization_barrier(jnp.sum(jnp.cumsum(onehot, axis=2, dtype=jnp.int32) * onehot, axis=-1, dtype=jnp.int32)) - 1
    shard_ids = jnp.broadcast_to(jnp.arange(SHARDS, dtype=jnp.int32)[None, :, None], destination.shape)
    source_ids = jnp.broadcast_to(jnp.arange(LOADERS, dtype=jnp.int32)[:, None, None], destination.shape)
    slot_read = jnp.minimum(slot, CAP - 1).astype(jnp.int32)

    def one_sequence(output_acc, sequence_id):
        chosen = destination == sequence_id
        slot_write = jnp.where(chosen, slot, CAP).astype(jnp.int32)

        def table(values_in, dtype):
            empty = jnp.zeros((SHARDS, LOADERS, CAP) + values_in.shape[3:], dtype)
            return empty.at[shard_ids, source_ids, slot_write].set(values_in, mode='drop')
        table_query = table(queries, jnp.bfloat16)
        table_key = table(key_rows, jnp.bfloat16)
        table_value = table(value_rows, jnp.bfloat16)
        table_live = table(jnp.ones_like(destination), jnp.int32)
        table_start = table(doc_starts, jnp.int32)
        normed = attend_sequence(table_query, table_key, table_value, table_live, table_start, decay_rate, norm_gain)
        rows_back = normed[shard_ids, source_ids, slot_read]
        return (jnp.where(chosen[..., None, None], rows_back, output_acc), None)
    initial = jnp.zeros(queries.shape, jnp.bfloat16)
    attended, unused = lax.scan(one_sequence, initial, jnp.arange(LOADERS, dtype=jnp.int32))
    return attended
```

```python
import functools
import jax
import jax.numpy as jnp
from jax import lax
from jax.experimental import pallas as pl
from jax.experimental.pallas import tpu as pltpu
from jax.sharding import PartitionSpec as P

MESH = pl.DeviceIdType.MESH
F32 = jnp.float32
BF16 = jnp.bfloat16
eps_norm = 1e-06
HG = 4
HC = 2
ZT = jnp.float32
ZLAG = 4


def update_kernel(seqs, cap, k_ref, v_ref, kw_ref, u_ref):
    d = u_ref.shape[-1]

    def body(g, _):
        rows = pl.ds(pl.multiple_of(g * cap, 16), cap)
        weight = kw_ref[0, rows, :]
        for j in range(HG):
            cols = slice(j * d, (j + 1) * d)
            scaled = (k_ref[rows, cols].astype(F32) * weight[:, j : j + 1]).astype(BF16)
            update = lax.dot_general(
                scaled, v_ref[rows, cols], (((0,), (0,)), ((), ())), preferred_element_type=F32
            )
            u_ref[pl.ds(g, 1), j] = update.astype(BF16)[None]
        return 0

    lax.fori_loop(0, seqs, body, 0)


def updates_of(key_packed, value_packed, key_weight, seqs, cap, heads, d):
    total = seqs * cap
    kw = key_weight.reshape(total, heads // HG, HG).transpose(1, 0, 2)
    return pl.pallas_call(
        functools.partial(update_kernel, seqs, cap),
        grid=(heads // HG,),
        out_shape=jax.ShapeDtypeStruct((seqs, heads, d, d), BF16),
        in_specs=[
            pl.BlockSpec((total, HG * d), lambda i: (0, i)),
            pl.BlockSpec((total, HG * d), lambda i: (0, i)),
            pl.BlockSpec((1, total, HG), lambda i: (i, 0, 0)),
        ],
        out_specs=pl.BlockSpec((seqs, HG, d, d), lambda i: (0, i, 0, 0)),
    )(key_packed, value_packed, kw)


def scan_kernel(levels, shards, seqs, heads, *refs):
    dec_ref, u_ref, out_ref = refs[:3]
    cur = [u_ref] + list(refs[3 : 3 + levels - 1])
    refs = refs[2 + levels :]
    got = refs[:levels]
    put = refs[levels : 2 * levels]
    total, zin = refs[2 * levels : 2 * levels + 2]
    up_s, up_r, dn_s, dn_r, z_s, z_r = refs[2 * levels + 2 :]
    me = lax.axis_index("dp")
    shard = lax.axis_index("seq")
    chunks = heads // HC

    def bit(k):
        return lax.rem(lax.div(me, 2**k), 2)

    def partner(k):
        return me + 2**k - bit(k) * (2 ** (k + 1))

    def low(k):
        return lax.rem(me, 2**k)

    def decay(table, seq, head):
        return dec_ref[(table * seqs + seq) * heads + head]

    barrier = pltpu.get_barrier_semaphore()
    for k in range(levels):
        pl.semaphore_signal(barrier, inc=1, device_id=(partner(k), shard), device_id_type=MESH)

    @pl.when(shard > 0)
    def _():
        pl.semaphore_signal(barrier, inc=1, device_id=(me, shard - 1), device_id_type=MESH)

    @pl.when(shard < shards - 1)
    def _():
        pl.semaphore_signal(barrier, inc=1, device_id=(me, shard + 1), device_id_type=MESH)

    ends = (shard > 0).astype(jnp.int32) + (shard < shards - 1).astype(jnp.int32)
    pl.semaphore_wait(barrier, levels + ends)

    @pl.when(shard == 0)
    def _():
        def clear(i, _):
            zin[pl.ds(i, 1)] = jnp.zeros((1,) + zin.shape[1:], zin.dtype)
            return 0

        lax.fori_loop(0, heads, clear, 0)

    def part(c):
        return pl.ds(c * HC, HC)

    def up_copy(k, c):
        return pltpu.make_async_remote_copy(
            src_ref=cur[k].at[:, 1 - bit(k), part(c)],
            dst_ref=got[k].at[:, part(c)],
            send_sem=up_s.at[k, c],
            recv_sem=up_r.at[k, c],
            device_id=(partner(k), shard),
            device_id_type=MESH,
        )

    def down_copy(k, c, j, receive):
        owner = partner(k) if receive else me
        seq = j * 2 ** (k + 1) + lax.rem(owner, 2 ** (k + 1))
        slot = 2 ** (levels - k - 1) - 1 + j
        return pltpu.make_async_remote_copy(
            src_ref=put[k].at[j, part(c)],
            dst_ref=out_ref.at[seq, part(c)],
            send_sem=dn_s.at[slot, c],
            recv_sem=dn_r.at[slot, c],
            device_id=(partner(k), shard),
            device_id_type=MESH,
        )

    def z_copy(c, target):
        return pltpu.make_async_remote_copy(
            src_ref=total.at[part(c)],
            dst_ref=zin.at[part(c)],
            send_sem=z_s.at[c],
            recv_sem=z_r.at[c],
            device_id=(me, target),
            device_id_type=MESH,
        )

    def up(k, c):
        up_copy(k, c).wait_recv()
        mine = bit(k)
        first = (mine == 0).astype(F32)
        share = 2 ** (levels - k - 1)

        def body(i, _):
            j, head = lax.div(i, HC), c * HC + lax.rem(i, HC)
            seq = j * 2 ** (k + 1) + low(k + 1)
            own = cur[k][j, mine, head].astype(F32)
            other = got[k][j, head].astype(F32)
            hi = decay(k, seq, head)
            own_w = first * hi + (1.0 - first)
            other_w = first + (1.0 - first) * hi
            both = own * own_w + other * other_w
            if k + 1 < levels:
                cur[k + 1][lax.div(j, 2), lax.rem(j, 2), head] = both.astype(BF16)
            else:
                total[head] = both.astype(total.dtype)
            return 0

        lax.fori_loop(0, share * HC, body, 0)
        if k + 1 < levels:
            up_copy(k + 1, c).start()

    def across(c):
        @pl.when(shard > 0)
        def _():
            z_copy(c, shard).wait_recv()

        def body(i, _):
            head = c * HC + i
            state = zin[head]
            out_ref[me, head] = state.astype(BF16)
            nxt = state.astype(F32) * decay(2 * levels, me, head) + total[head].astype(F32)
            total[head] = nxt.astype(total.dtype)
            return 0

        lax.fori_loop(0, HC, body, 0)

        @pl.when(shard < shards - 1)
        def _():
            z_copy(c, shard + 1).start()

    def down(k, c):
        if k + 1 < levels:
            for j in range(2 ** (levels - k - 2)):
                down_copy(k + 1, c, j, True).wait_recv()
        mine = bit(k)
        first = (mine == 0).astype(F32)
        share = 2 ** (levels - k - 1)

        def body(i, _):
            j, head = lax.div(i, HC), c * HC + lax.rem(i, HC)
            seq = j * 2 ** (k + 1) + low(k + 1)
            base = out_ref[seq, head].astype(F32)
            own = cur[k][j, mine, head].astype(F32)
            other = got[k][j, head].astype(F32)
            lo = first * own + (1.0 - first) * other
            later = base * decay(levels + k, seq, head) + lo
            out_ref[seq, head] = (first * base + (1.0 - first) * later).astype(BF16)
            put[k][j, head] = (first * later + (1.0 - first) * base).astype(BF16)
            return 0

        lax.fori_loop(0, share * HC, body, 0)
        for j in range(share):
            down_copy(k, c, j, False).start()

    for c in range(chunks):
        up_copy(0, c).start()
    z_lag = levels - 1 + ZLAG
    for t in range(chunks + z_lag + levels + 1):
        for k in range(levels):
            if 0 <= t - k < chunks:
                up(k, t - k)
        if 0 <= t - z_lag < chunks:
            across(t - z_lag)
        for k in range(levels - 1, -1, -1):
            c = t - z_lag - (levels - 1 - k)
            if 0 <= c < chunks:
                down(k, c)
    for c in range(chunks):
        for j in range(2 ** (levels - 1)):
            down_copy(0, c, j, True).wait_recv()
        for k in range(levels):
            up_copy(k, c).wait_send()
            for j in range(2 ** (levels - k - 1)):
                down_copy(k, c, j, False).wait_send()

    @pl.when(shard < shards - 1)
    def _():
        for c in range(chunks):
            z_copy(c, shard + 1).wait_send()


def scan_states(decays, updates, levels, shards, call):
    seqs, heads, d = updates.shape[:3]
    chunks = heads // HC
    vm = pltpu.VMEM
    share = [2 ** (levels - k - 1) for k in range(levels)]
    dma = pltpu.SemaphoreType.DMA
    return pl.pallas_call(
        functools.partial(scan_kernel, levels, shards, seqs, heads),
        out_shape=jax.ShapeDtypeStruct((seqs, heads, d, d), BF16),
        in_specs=[
            pl.BlockSpec(memory_space=pltpu.SMEM),
            pl.BlockSpec(memory_space=pltpu.VMEM),
        ],
        out_specs=pl.BlockSpec(memory_space=pltpu.VMEM),
        scratch_shapes=[vm((share[k], 2, heads, d, d), BF16) for k in range(1, levels)]
        + [vm((share[k], heads, d, d), BF16) for k in range(levels)]
        + [vm((share[k], heads, d, d), BF16) for k in range(levels)]
        + [vm((heads, d, d), ZT), vm((heads, d, d), ZT)]
        + [dma((levels, chunks)), dma((levels, chunks))]
        + [dma((seqs - 1, chunks)), dma((seqs - 1, chunks))]
        + [dma((chunks,)), dma((chunks,))],
        compiler_params=pltpu.CompilerParams(
            collective_id=call, has_side_effects=True, vmem_limit_bytes=60 * 1024 * 1024
        ),
    )(decays, updates.reshape(seqs // 2, 2, heads, d, d))


def finish_kernel(
    heads, d, rate_ref, q_ref, k_ref, v_ref, state_ref, col_ref, row_ref, cw_ref, gain_ref, o_ref, mixed
):
    cap = q_ref.shape[0]
    ri = lax.broadcasted_iota(jnp.int32, (cap, cap), 0)
    ci = lax.broadcasted_iota(jnp.int32, (cap, cap), 1)
    keep = (ri >= ci) & (col_ref[...] == row_ref[0])
    gap = jnp.maximum(ri - ci, 0).astype(F32)
    carry = cw_ref[...]
    squares = jnp.zeros((cap, d), F32)
    for h in range(heads):
        cols = slice(h * d, (h + 1) * d)
        q = q_ref[:, cols]
        scores = lax.dot_general(
            q, k_ref[:, cols], (((1,), (1,)), ((), ())), preferred_element_type=F32
        )
        weight = jnp.where(keep, jnp.exp(-rate_ref[h] * gap), 0.0)
        half = (scores * weight).astype(BF16)
        intra = jnp.dot(half, v_ref[:, cols], preferred_element_type=F32)
        inter = jnp.dot(q, state_ref[0, h], preferred_element_type=F32)
        out = intra + inter * carry[:, h : h + 1]
        mixed[:, cols] = out
        squares = squares + out * out
    mean = jnp.sum(squares, axis=1, keepdims=True) * (1.0 / (heads * d))
    scale = lax.rsqrt(mean + eps_norm)
    for h in range(heads):
        cols = slice(h * d, (h + 1) * d)
        o_ref[:, cols] = (mixed[:, cols] * scale * gain_ref[:, cols]).astype(BF16)


def finish(rate, query, key, value, states, doc, carry_weight, gain, seqs, cap, heads, d):
    total = seqs * cap
    wide = pl.BlockSpec((cap, heads * d), lambda g: (g, 0))
    return pl.pallas_call(
        functools.partial(finish_kernel, heads, d),
        grid=(seqs,),
        out_shape=jax.ShapeDtypeStruct((total, heads * d), BF16),
        in_specs=[
            pl.BlockSpec(memory_space=pltpu.SMEM),
            wide,
            wide,
            wide,
            pl.BlockSpec((1, heads, d, d), lambda g: (g, 0, 0, 0)),
            pl.BlockSpec((cap, 1), lambda g: (g, 0)),
            pl.BlockSpec((1, 1, cap), lambda g: (g, 0, 0)),
            pl.BlockSpec((cap, heads), lambda g: (g, 0)),
            pl.BlockSpec((1, heads * d), lambda g: (0, 0)),
        ],
        out_specs=wide,
        scratch_shapes=[pltpu.VMEM((cap, heads * d), F32)],
    )(
        rate,
        query,
        key,
        value,
        states,
        doc.reshape(total, 1),
        doc.reshape(seqs, 1, cap),
        carry_weight,
        gain.reshape(1, heads * d),
    )


def per_device(queries, key_rows, value_rows, destination, doc_starts, decay_rate, norm_gain):
    loaders = lax.axis_size("dp")
    shards = lax.axis_size("seq")
    rows, heads, d = queries.shape[2:]
    cap = 3 * rows // (2 * loaders)
    levels = loaders.bit_length() - 1
    total = loaders * cap
    dest = destination[0, 0]
    start = doc_starts[0, 0]
    r = jnp.arange(rows, dtype=jnp.int32)
    earlier = (dest[:, None] == dest[None, :]) & (r[None, :] < r[:, None])
    slot = jnp.sum(earlier.astype(jnp.int32), axis=1)
    flat = dest * cap + slot
    place = jnp.arange(total, dtype=jnp.int32)
    hit = place[:, None] == flat[None, :]
    source = jnp.sum(jnp.where(hit, r[None, :], 0), axis=1)
    begin = jnp.sum(jnp.where(hit, start[None, :], 0), axis=1).reshape(loaders, cap)
    targets = jnp.arange(loaders, dtype=jnp.int32)
    number = jnp.sum((dest[None, :] == targets[:, None]).astype(jnp.int32), axis=1)
    position = jnp.arange(cap, dtype=jnp.int32)
    upto = (position[None, :] <= position[:, None]).astype(jnp.int32)
    doc = jnp.sum(begin[:, None, :] * upto[None], axis=2)
    doc_end = jnp.sum(begin, axis=1)

    facts = lax.all_gather(jnp.stack([number, doc_end]), "dp", axis=0)
    me = lax.axis_index("dp")

    def span_decay(first, size):
        inside = ((targets >= first) & (targets < first + size)).astype(jnp.int32)
        span, docs = jnp.sum(facts * inside[:, None, None], axis=0)
        gone = jnp.exp(-decay_rate[None, :] * span.astype(F32)[:, None])
        return jnp.where((docs == 0)[:, None], gone, 0.0)

    tables = []
    for side in (1, 0):
        for k in range(levels):
            tables.append(span_decay((me // 2 ** (k + 1) * 2 + side) * 2**k, 2**k))
    tables.append(span_decay(0, loaders))
    tables = jnp.stack(tables)

    until = jnp.maximum(number[:, None] - 1 - position[None, :], 0).astype(F32)
    key_keep = (position[None, :] < number[:, None]) & (doc == doc_end[:, None])
    key_weight = jnp.where(
        key_keep[:, :, None], jnp.exp(-decay_rate[None, None, :] * until[:, :, None]), 0.0
    ).reshape(total, heads)
    since = (position + 1).astype(F32)
    carry_weight = jnp.where(
        (doc == 0)[:, :, None], jnp.exp(-decay_rate[None, None, :] * since[None, :, None]), 0.0
    ).reshape(total, heads)

    def pack(rows_in):
        return rows_in[0, 0].reshape(rows, heads * d)[source]

    key, value, query = pack(key_rows), pack(value_rows), pack(queries)
    updates = updates_of(key, value, key_weight, loaders, cap, heads, d)
    passes = max(1, loaders // 8)
    width = heads // passes
    states = [
        scan_states(
            tables[:, :, i * width : (i + 1) * width].reshape(-1),
            updates[:, i * width : (i + 1) * width],
            levels,
            shards,
            i,
        )
        for i in range(passes)
    ]
    states = states[0] if passes == 1 else jnp.concatenate(states, axis=1)
    packed = finish(
        decay_rate, query, key, value, states, doc, carry_weight, norm_gain, loaders, cap, heads, d
    )
    return packed[flat].reshape(1, 1, rows, heads, d)


def solution(mesh):
    placed = (
        P("dp", "seq", None, None, None),
        P("dp", "seq", None, None, None),
        P("dp", "seq", None, None, None),
        P("dp", "seq", None),
        P("dp", "seq", None),
        P(),
        P(),
    )
    return jax.shard_map(
        per_device,
        mesh=mesh,
        in_specs=placed,
        out_specs=P("dp", "seq", None, None, None),
        check_vma=False,
    )
```

```python
import functools
import jax
import jax.numpy as jnp
from jax import lax
from jax.experimental import pallas as pl
from jax.experimental.pallas import tpu as pltpu
from jax.sharding import PartitionSpec as P

MESH = pl.DeviceIdType.MESH
F32 = jnp.float32
BF16 = jnp.bfloat16
eps_norm = 1e-06
HG = 8
HO = 16
HC = 2
ZT = jnp.float32
ZLAG = 4


def update_kernel(seqs, cap, flat_ref, k_ref, v_ref, q_ref, kw_ref, u_ref, ko, vo, qo, hot, tall, wide):
    d = u_ref.shape[-1]
    rows = k_ref.shape[0]

    @pl.when(pl.program_id(0) == 0)
    def _():
        place = lax.broadcasted_iota(jnp.int32, hot.shape, 0)
        hot[...] = jnp.where(place == flat_ref[...], 1.0, 0.0).astype(BF16)

    for x_ref, o_ref in ((k_ref, ko), (v_ref, vo), (q_ref, qo)):
        tall[...] = x_ref[...].astype(F32).reshape(rows * HG, d)
        for j in range(HG):
            wide[:, j * d : (j + 1) * d] = tall[pl.ds(j, rows, stride=HG), :].astype(BF16)
        for j in range(HG // 2):
            cols = slice(2 * j * d, 2 * (j + 1) * d)
            moved = jnp.dot(hot[...], wide[:, cols], preferred_element_type=F32)
            o_ref[:, cols] = moved.astype(BF16)

    def body(g, _):
        here = pl.ds(pl.multiple_of(g * cap, 16), cap)
        weight = kw_ref[0, here, :]
        for j in range(HG):
            cols = slice(j * d, (j + 1) * d)
            scaled = (ko[here, cols].astype(F32) * weight[:, j : j + 1]).astype(BF16)
            update = lax.dot_general(
                scaled, vo[here, cols], (((0,), (0,)), ((), ())), preferred_element_type=F32
            )
            u_ref[pl.ds(g, 1), j] = update.astype(BF16)[None]
        return 0

    lax.fori_loop(0, seqs, body, 0)


def updates_of(flat, key, value, query, key_weight, seqs, cap):
    rows, heads, d = key.shape
    total = seqs * cap
    kw = key_weight.reshape(total, heads // HG, HG).transpose(1, 0, 2)
    natural = pl.BlockSpec((rows, HG, d), lambda i: (0, i, 0))
    packed = pl.BlockSpec((total, HG * d), lambda i: (0, i))
    packed_shape = jax.ShapeDtypeStruct((total, heads * d), BF16)
    return pl.pallas_call(
        functools.partial(update_kernel, seqs, cap),
        grid=(heads // HG,),
        out_shape=[jax.ShapeDtypeStruct((seqs, heads, d, d), BF16)] + [packed_shape] * 3,
        in_specs=[
            pl.BlockSpec((1, rows), lambda i: (0, 0)),
            natural,
            natural,
            natural,
            pl.BlockSpec((1, total, HG), lambda i: (i, 0, 0)),
        ],
        out_specs=[pl.BlockSpec((seqs, HG, d, d), lambda i: (0, i, 0, 0)), packed, packed, packed],
        scratch_shapes=[
            pltpu.VMEM((total, rows), BF16),
            pltpu.VMEM((rows * HG, d), F32),
            pltpu.VMEM((rows, HG * d), BF16),
        ],
        compiler_params=pltpu.CompilerParams(vmem_limit_bytes=56 * 1024 * 1024),
    )(flat.reshape(1, rows), key, value, query, kw)


def scan_kernel(levels, shards, seqs, heads, *refs):
    fact_ref, rate_ref, u_ref, out_ref = refs[:4]
    cur = [u_ref] + list(refs[4 : 4 + levels - 1])
    facts, dec, f_s, f_r = refs[3 + levels : 7 + levels]
    refs = refs[7 + levels :]
    got = refs[:levels]
    put = refs[levels : 2 * levels]
    total, zin = refs[2 * levels : 2 * levels + 2]
    up_s, up_r, dn_s, dn_r, z_s, z_r = refs[2 * levels + 2 :]
    me = lax.axis_index("dp")
    shard = lax.axis_index("seq")
    chunks = heads // HC

    def bit(k):
        return lax.rem(lax.div(me, 2**k), 2)

    def partner(k):
        return me + 2**k - bit(k) * (2 ** (k + 1))

    def low(k):
        return lax.rem(me, 2**k)

    def decay(table, seq, head):
        return dec[table * seqs + seq, pl.ds(head, 1), :]

    barrier = pltpu.get_barrier_semaphore()
    for i in range(1, seqs):
        peer = lax.rem(me + i, seqs)
        pl.semaphore_signal(barrier, inc=1, device_id=(peer, shard), device_id_type=MESH)

    @pl.when(shard > 0)
    def _():
        pl.semaphore_signal(barrier, inc=1, device_id=(me, shard - 1), device_id_type=MESH)

    @pl.when(shard < shards - 1)
    def _():
        pl.semaphore_signal(barrier, inc=1, device_id=(me, shard + 1), device_id_type=MESH)

    ends = (shard > 0).astype(jnp.int32) + (shard < shards - 1).astype(jnp.int32)
    pl.semaphore_wait(barrier, seqs - 1 + ends)

    @pl.when(shard == 0)
    def _():
        def clear(i, _):
            zin[pl.ds(i, 1)] = jnp.zeros((1,) + zin.shape[1:], zin.dtype)
            return 0

        lax.fori_loop(0, heads, clear, 0)

    def part(c):
        return pl.ds(c * HC, HC)

    def up_copy(k, c):
        return pltpu.make_async_remote_copy(
            src_ref=cur[k].at[:, 1 - bit(k), part(c)],
            dst_ref=got[k].at[:, part(c)],
            send_sem=up_s.at[k, c],
            recv_sem=up_r.at[k, c],
            device_id=(partner(k), shard),
            device_id_type=MESH,
        )

    def down_copy(k, c, j, receive):
        owner = partner(k) if receive else me
        seq = j * 2 ** (k + 1) + lax.rem(owner, 2 ** (k + 1))
        slot = 2 ** (levels - k - 1) - 1 + j
        return pltpu.make_async_remote_copy(
            src_ref=put[k].at[j, part(c)],
            dst_ref=out_ref.at[seq, part(c)],
            send_sem=dn_s.at[slot, c],
            recv_sem=dn_r.at[slot, c],
            device_id=(partner(k), shard),
            device_id_type=MESH,
        )

    def z_copy(c, target):
        return pltpu.make_async_remote_copy(
            src_ref=total.at[part(c)],
            dst_ref=zin.at[part(c)],
            send_sem=z_s.at[c],
            recv_sem=z_r.at[c],
            device_id=(me, target),
            device_id_type=MESH,
        )

    def up(k, c):
        up_copy(k, c).wait_recv()
        mine = bit(k)
        first = (mine == 0).astype(F32)
        share = 2 ** (levels - k - 1)

        def body(i, _):
            j, head = lax.div(i, HC), c * HC + lax.rem(i, HC)
            seq = j * 2 ** (k + 1) + low(k + 1)
            own = cur[k][j, mine, head].astype(F32)
            other = got[k][j, head].astype(F32)
            hi = decay(k, seq, head)
            own_w = first * hi + (1.0 - first)
            other_w = first + (1.0 - first) * hi
            both = own * own_w + other * other_w
            if k + 1 < levels:
                cur[k + 1][lax.div(j, 2), lax.rem(j, 2), head] = both.astype(BF16)
            else:
                total[head] = both.astype(total.dtype)
            return 0

        lax.fori_loop(0, share * HC, body, 0)
        if k + 1 < levels:
            up_copy(k + 1, c).start()

    def across(c):
        @pl.when(shard > 0)
        def _():
            z_copy(c, shard).wait_recv()

        def body(i, _):
            head = c * HC + i
            state = zin[head]
            out_ref[me, head] = state.astype(BF16)
            nxt = state.astype(F32) * decay(2 * levels, me, head) + total[head].astype(F32)
            total[head] = nxt.astype(total.dtype)
            return 0

        lax.fori_loop(0, HC, body, 0)

        @pl.when(shard < shards - 1)
        def _():
            z_copy(c, shard + 1).start()

    def down(k, c):
        if k + 1 < levels:
            for j in range(2 ** (levels - k - 2)):
                down_copy(k + 1, c, j, True).wait_recv()
        mine = bit(k)
        first = (mine == 0).astype(F32)
        share = 2 ** (levels - k - 1)

        def body(i, _):
            j, head = lax.div(i, HC), c * HC + lax.rem(i, HC)
            seq = j * 2 ** (k + 1) + low(k + 1)
            base = out_ref[seq, head].astype(F32)
            own = cur[k][j, mine, head].astype(F32)
            other = got[k][j, head].astype(F32)
            lo = first * own + (1.0 - first) * other
            later = base * decay(levels + k, seq, head) + lo
            out_ref[seq, head] = (first * base + (1.0 - first) * later).astype(BF16)
            put[k][j, head] = (first * later + (1.0 - first) * base).astype(BF16)
            return 0

        lax.fori_loop(0, share * HC, body, 0)
        for j in range(share):
            down_copy(k, c, j, False).start()

    def fact_copy(i):
        return pltpu.make_async_remote_copy(
            src_ref=fact_ref,
            dst_ref=facts.at[me],
            send_sem=f_s.at[i - 1],
            recv_sem=f_r.at[i - 1],
            device_id=(lax.rem(me + i, seqs), shard),
            device_id_type=MESH,
        )

    def fact_arrival(i):
        return pltpu.make_async_remote_copy(
            src_ref=fact_ref,
            dst_ref=facts.at[lax.rem(me + seqs - i, seqs)],
            send_sem=f_s.at[i - 1],
            recv_sem=f_r.at[i - 1],
            device_id=(lax.rem(me + i, seqs), shard),
            device_id_type=MESH,
        )

    for i in range(1, seqs):
        fact_copy(i).start()
    for c in range(chunks):
        up_copy(0, c).start()
    facts[pl.ds(me, 1)] = fact_ref[...][None]
    for i in range(1, seqs):
        fact_arrival(i).wait_recv()
    rate = rate_ref[...]
    spans = [((me // 2 ** (k + 1) * 2 + 1) * 2**k, 2**k) for k in range(levels)]
    spans += [((me // 2 ** (k + 1) * 2) * 2**k, 2**k) for k in range(levels)]
    spans += [(me * 0, seqs)]
    for table, (begin, size) in enumerate(spans):
        count = jnp.zeros(fact_ref.shape[1:], F32)
        docs = jnp.zeros(fact_ref.shape[1:], F32)
        for loader in range(seqs):
            inside = ((loader >= begin) & (loader < begin + size)).astype(F32)
            count = count + facts[loader, 0] * inside
            docs = docs + facts[loader, 1] * inside
        for seq in range(seqs):
            gone = jnp.exp(-rate * count[seq : seq + 1])
            dec[table * seqs + seq] = jnp.where(docs[seq : seq + 1] == 0.0, gone, 0.0)
    z_lag = levels - 1 + ZLAG
    for t in range(chunks + z_lag + levels + 1):
        for k in range(levels):
            if 0 <= t - k < chunks:
                up(k, t - k)
        if 0 <= t - z_lag < chunks:
            across(t - z_lag)
        for k in range(levels - 1, -1, -1):
            c = t - z_lag - (levels - 1 - k)
            if 0 <= c < chunks:
                down(k, c)
    for c in range(chunks):
        for j in range(2 ** (levels - 1)):
            down_copy(0, c, j, True).wait_recv()
        for k in range(levels):
            up_copy(k, c).wait_send()
            for j in range(2 ** (levels - k - 1)):
                down_copy(k, c, j, False).wait_send()

    for i in range(1, seqs):
        fact_copy(i).wait_send()

    @pl.when(shard < shards - 1)
    def _():
        for c in range(chunks):
            z_copy(c, shard + 1).wait_send()


def scan_states(facts, rate, updates, levels, shards, call):
    seqs, heads, d = updates.shape[:3]
    chunks = heads // HC
    vm = pltpu.VMEM
    share = [2 ** (levels - k - 1) for k in range(levels)]
    dma = pltpu.SemaphoreType.DMA
    return pl.pallas_call(
        functools.partial(scan_kernel, levels, shards, seqs, heads),
        out_shape=jax.ShapeDtypeStruct((seqs, heads, d, d), BF16),
        in_specs=[
            pl.BlockSpec(memory_space=pltpu.VMEM),
            pl.BlockSpec(memory_space=pltpu.VMEM),
            pl.BlockSpec(memory_space=pltpu.VMEM),
        ],
        out_specs=pl.BlockSpec(memory_space=pltpu.VMEM),
        scratch_shapes=[vm((share[k], 2, heads, d, d), BF16) for k in range(1, levels)]
        + [vm((seqs,) + facts.shape, F32), vm(((2 * levels + 1) * seqs, heads, d), F32)]
        + [dma((seqs - 1,)), dma((seqs - 1,))]
        + [vm((share[k], heads, d, d), BF16) for k in range(levels)]
        + [vm((share[k], heads, d, d), BF16) for k in range(levels)]
        + [vm((heads, d, d), ZT), vm((heads, d, d), ZT)]
        + [dma((levels, chunks)), dma((levels, chunks))]
        + [dma((seqs - 1, chunks)), dma((seqs - 1, chunks))]
        + [dma((chunks,)), dma((chunks,))],
        compiler_params=pltpu.CompilerParams(
            collective_id=call, has_side_effects=True, vmem_limit_bytes=60 * 1024 * 1024
        ),
    )(facts, rate, updates.reshape(seqs // 2, 2, heads, d, d))


def finish_kernel(
    heads, d, rate_ref, flat_ref, q_ref, k_ref, v_ref, state_ref, col_ref, row_ref, cw_ref, gain_ref,
    o_ref, mixed, normed, tall
):
    cap = q_ref.shape[0]
    g = pl.program_id(0)
    ri = lax.broadcasted_iota(jnp.int32, (cap, cap), 0)
    ci = lax.broadcasted_iota(jnp.int32, (cap, cap), 1)
    keep = (ri >= ci) & (col_ref[...] == row_ref[0])
    gap = jnp.maximum(ri - ci, 0).astype(F32)
    carry = cw_ref[...]
    squares = jnp.zeros((cap, d), F32)
    for h in range(heads):
        cols = slice(h * d, (h + 1) * d)
        q = q_ref[:, cols]
        scores = lax.dot_general(
            q, k_ref[:, cols], (((1,), (1,)), ((), ())), preferred_element_type=F32
        )
        weight = jnp.where(keep, jnp.exp(-rate_ref[h] * gap), 0.0)
        half = (scores * weight).astype(BF16)
        intra = jnp.dot(half, v_ref[:, cols], preferred_element_type=F32)
        inter = jnp.dot(q, state_ref[0, h], preferred_element_type=F32)
        out = intra + inter * carry[:, h : h + 1]
        mixed[:, cols] = out
        squares = squares + out * out
    mean = jnp.sum(squares, axis=1, keepdims=True) * (1.0 / (heads * d))
    scale = lax.rsqrt(mean + eps_norm)
    for h in range(heads):
        cols = slice(h * d, (h + 1) * d)
        result = (mixed[:, cols] * scale * gain_ref[:, cols]).astype(BF16)
        normed[pl.ds(pl.multiple_of(g * cap, 16), cap), cols] = result

    @pl.when(g == pl.num_programs(0) - 1)
    def _():
        rows, total = o_ref.shape[0], normed.shape[0]
        place = lax.broadcasted_iota(jnp.int32, (rows, total), 1)
        hot = jnp.where(place == flat_ref[...], 1.0, 0.0).astype(BF16)
        for i in range(heads // HO):
            for j in range(0, HO, 2):
                h = i * HO + j
                back = jnp.dot(hot, normed[:, h * d : (h + 2) * d], preferred_element_type=F32)
                tall[pl.ds(j, rows, stride=HO), :] = back[:, :d]
                tall[pl.ds(j + 1, rows, stride=HO), :] = back[:, d:]
            o_ref[:, i * HO : (i + 1) * HO, :] = tall[...].reshape(rows, HO, d).astype(BF16)


def finish(rate, flat, query, key, value, states, doc, carry_weight, gain, seqs, cap, heads, d):
    total = seqs * cap
    rows = flat.shape[0]
    wide = pl.BlockSpec((cap, heads * d), lambda g: (g, 0))
    return pl.pallas_call(
        functools.partial(finish_kernel, heads, d),
        grid=(seqs,),
        out_shape=jax.ShapeDtypeStruct((rows, heads, d), BF16),
        in_specs=[
            pl.BlockSpec(memory_space=pltpu.SMEM),
            pl.BlockSpec((rows, 1), lambda g: (0, 0)),
            wide,
            wide,
            wide,
            pl.BlockSpec((1, heads, d, d), lambda g: (g, 0, 0, 0)),
            pl.BlockSpec((cap, 1), lambda g: (g, 0)),
            pl.BlockSpec((1, 1, cap), lambda g: (g, 0, 0)),
            pl.BlockSpec((cap, heads), lambda g: (g, 0)),
            pl.BlockSpec((1, heads * d), lambda g: (0, 0)),
        ],
        out_specs=pl.BlockSpec((rows, heads, d), lambda g: (0, 0, 0)),
        scratch_shapes=[
            pltpu.VMEM((cap, heads * d), F32),
            pltpu.VMEM((total, heads * d), BF16),
            pltpu.VMEM((rows * HO, d), F32),
        ],
        compiler_params=pltpu.CompilerParams(vmem_limit_bytes=56 * 1024 * 1024),
    )(
        rate,
        flat.reshape(rows, 1),
        query,
        key,
        value,
        states,
        doc.reshape(total, 1),
        doc.reshape(seqs, 1, cap),
        carry_weight,
        gain.reshape(1, heads * d),
    )


def per_device(queries, key_rows, value_rows, destination, doc_starts, decay_rate, norm_gain):
    loaders = lax.axis_size("dp")
    shards = lax.axis_size("seq")
    rows, heads, d = queries.shape[2:]
    cap = 3 * rows // (2 * loaders)
    levels = loaders.bit_length() - 1
    total = loaders * cap
    dest = destination[0, 0]
    start = doc_starts[0, 0]
    r = jnp.arange(rows, dtype=jnp.int32)
    earlier = (dest[:, None] == dest[None, :]) & (r[None, :] < r[:, None])
    slot = jnp.sum(earlier.astype(jnp.int32), axis=1)
    flat = dest * cap + slot
    place = jnp.arange(total, dtype=jnp.int32)
    hit = place[:, None] == flat[None, :]
    begin = jnp.sum(jnp.where(hit, start[None, :], 0), axis=1).reshape(loaders, cap)
    targets = jnp.arange(loaders, dtype=jnp.int32)
    number = jnp.sum((dest[None, :] == targets[:, None]).astype(jnp.int32), axis=1)
    position = jnp.arange(cap, dtype=jnp.int32)
    upto = (position[None, :] <= position[:, None]).astype(jnp.int32)
    doc = jnp.sum(begin[:, None, :] * upto[None], axis=2)
    doc_end = jnp.sum(begin, axis=1)

    facts = jnp.broadcast_to(jnp.stack([number, doc_end]).astype(F32)[:, :, None], (2, loaders, d))
    rate = jnp.broadcast_to(decay_rate[:, None], (heads, d))

    until = jnp.maximum(number[:, None] - 1 - position[None, :], 0).astype(F32)
    key_keep = (position[None, :] < number[:, None]) & (doc == doc_end[:, None])
    key_weight = jnp.where(
        key_keep[:, :, None], jnp.exp(-decay_rate[None, None, :] * until[:, :, None]), 0.0
    ).reshape(total, heads)
    since = (position + 1).astype(F32)
    carry_weight = jnp.where(
        (doc == 0)[:, :, None], jnp.exp(-decay_rate[None, None, :] * since[None, :, None]), 0.0
    ).reshape(total, heads)

    updates, key, value, query = updates_of(
        flat, key_rows[0, 0], value_rows[0, 0], queries[0, 0], key_weight, loaders, cap
    )
    passes = max(1, loaders // 8)
    width = heads // passes
    states = [
        scan_states(
            facts,
            rate[i * width : (i + 1) * width],
            updates[:, i * width : (i + 1) * width],
            levels,
            shards,
            i,
        )
        for i in range(passes)
    ]
    states = states[0] if passes == 1 else jnp.concatenate(states, axis=1)
    attended = finish(
        decay_rate, flat, query, key, value, states, doc, carry_weight, norm_gain, loaders, cap, heads, d
    )
    return attended[None, None]


def solution(mesh):
    placed = (
        P("dp", "seq", None, None, None),
        P("dp", "seq", None, None, None),
        P("dp", "seq", None, None, None),
        P("dp", "seq", None),
        P("dp", "seq", None),
        P(),
        P(),
    )
    return jax.shard_map(
        per_device,
        mesh=mesh,
        in_specs=placed,
        out_specs=P("dp", "seq", None, None, None),
        check_vma=False,
    )
```

```python
import functools
import jax
import jax.numpy as jnp
from jax import lax
from jax.experimental import pallas as pl
from jax.experimental.pallas import tpu as pltpu
from jax.sharding import PartitionSpec as P

MESH = pl.DeviceIdType.MESH
F32 = jnp.float32
BF16 = jnp.bfloat16
eps_norm = 1e-06
HG = 8
HO = 16
HC = 2
ZT = jnp.float32
ZLAG = 4


def scan_kernel(levels, shards, seqs, heads, cap, *refs):
    fact_ref, rate_ref, flat_ref, k_ref, v_ref, q_ref, kw_ref, out_ref = refs[:8]
    packed = refs[8:11]
    refs = refs[11:]
    u_ref, hot, tall, wide, moved, pack_sem = refs[:6]
    refs = refs[6:]
    cur = [u_ref] + list(refs[: levels - 1])
    facts, dec, f_s, f_r = refs[levels - 1 : 3 + levels]
    refs = refs[3 + levels :]
    got = refs[:levels]
    put = got
    total, zin = refs[levels : levels + 2]
    up_s, up_r, dn_s, dn_r, z_s, z_r = refs[levels + 2 :]
    rows, _, d = k_ref.shape
    me = lax.axis_index("dp")
    shard = lax.axis_index("seq")
    chunks = heads // HC

    def bit(k):
        return lax.rem(lax.div(me, 2**k), 2)

    def partner(k):
        return me + 2**k - bit(k) * (2 ** (k + 1))

    def low(k):
        return lax.rem(me, 2**k)

    def decay(table, seq, head):
        return dec[table * seqs + seq, pl.ds(head, 1), :]

    barrier = pltpu.get_barrier_semaphore()
    for i in range(1, seqs):
        peer = lax.rem(me + i, seqs)
        pl.semaphore_signal(barrier, inc=1, device_id=(peer, shard), device_id_type=MESH)

    @pl.when(shard > 0)
    def _():
        pl.semaphore_signal(barrier, inc=1, device_id=(me, shard - 1), device_id_type=MESH)

    @pl.when(shard < shards - 1)
    def _():
        pl.semaphore_signal(barrier, inc=1, device_id=(me, shard + 1), device_id_type=MESH)

    ends = (shard > 0).astype(jnp.int32) + (shard < shards - 1).astype(jnp.int32)
    pl.semaphore_wait(barrier, seqs - 1 + ends)

    @pl.when(shard == 0)
    def _():
        def clear(i, _):
            zin[pl.ds(i, 1)] = jnp.zeros((1,) + zin.shape[1:], zin.dtype)
            return 0

        lax.fori_loop(0, heads, clear, 0)

    def part(c):
        return pl.ds(c * HC, HC)

    def up_copy(k, c):
        return pltpu.make_async_remote_copy(
            src_ref=cur[k].at[:, 1 - bit(k), part(c)],
            dst_ref=got[k].at[:, part(c)],
            send_sem=up_s.at[k, c],
            recv_sem=up_r.at[k, c],
            device_id=(partner(k), shard),
            device_id_type=MESH,
        )

    def down_copy(k, c, j, receive):
        owner = partner(k) if receive else me
        seq = j * 2 ** (k + 1) + lax.rem(owner, 2 ** (k + 1))
        slot = 2 ** (levels - k - 1) - 1 + j
        return pltpu.make_async_remote_copy(
            src_ref=put[k].at[j, part(c)],
            dst_ref=out_ref.at[seq, part(c)],
            send_sem=dn_s.at[slot, c],
            recv_sem=dn_r.at[slot, c],
            device_id=(partner(k), shard),
            device_id_type=MESH,
        )

    def z_copy(c, target):
        return pltpu.make_async_remote_copy(
            src_ref=total.at[part(c)],
            dst_ref=zin.at[part(c)],
            send_sem=z_s.at[c],
            recv_sem=z_r.at[c],
            device_id=(me, target),
            device_id_type=MESH,
        )

    def up(k, c):
        up_copy(k, c).wait_recv()
        mine = bit(k)
        first = (mine == 0).astype(F32)
        share = 2 ** (levels - k - 1)

        def body(i, _):
            j, head = lax.div(i, HC), c * HC + lax.rem(i, HC)
            seq = j * 2 ** (k + 1) + low(k + 1)
            own = cur[k][j, mine, head].astype(F32)
            other = got[k][j, head].astype(F32)
            hi = decay(k, seq, head)
            own_w = first * hi + (1.0 - first)
            other_w = first + (1.0 - first) * hi
            both = own * own_w + other * other_w
            if k + 1 < levels:
                cur[k + 1][lax.div(j, 2), lax.rem(j, 2), head] = both.astype(BF16)
            else:
                total[head] = both.astype(total.dtype)
            return 0

        lax.fori_loop(0, share * HC, body, 0)
        if k + 1 < levels:
            up_copy(k + 1, c).start()

    def across(c):
        @pl.when(shard > 0)
        def _():
            z_copy(c, shard).wait_recv()

        def body(i, _):
            head = c * HC + i
            state = zin[head]
            out_ref[me, head] = state.astype(BF16)
            nxt = state.astype(F32) * decay(2 * levels, me, head) + total[head].astype(F32)
            total[head] = nxt.astype(total.dtype)
            return 0

        lax.fori_loop(0, HC, body, 0)

        @pl.when(shard < shards - 1)
        def _():
            z_copy(c, shard + 1).start()

    def down(k, c):
        if k + 1 < levels:
            for j in range(2 ** (levels - k - 2)):
                down_copy(k + 1, c, j, True).wait_recv()
        mine = bit(k)
        first = (mine == 0).astype(F32)
        share = 2 ** (levels - k - 1)

        def body(i, _):
            j, head = lax.div(i, HC), c * HC + lax.rem(i, HC)
            seq = j * 2 ** (k + 1) + low(k + 1)
            base = out_ref[seq, head].astype(F32)
            own = cur[k][j, mine, head].astype(F32)
            other = got[k][j, head].astype(F32)
            lo = first * own + (1.0 - first) * other
            later = base * decay(levels + k, seq, head) + lo
            out_ref[seq, head] = (first * base + (1.0 - first) * later).astype(BF16)
            put[k][j, head] = (first * later + (1.0 - first) * base).astype(BF16)
            return 0

        lax.fori_loop(0, share * HC, body, 0)
        for j in range(share):
            down_copy(k, c, j, False).start()

    def fact_copy(i):
        return pltpu.make_async_remote_copy(
            src_ref=fact_ref,
            dst_ref=facts.at[me],
            send_sem=f_s.at[i - 1],
            recv_sem=f_r.at[i - 1],
            device_id=(lax.rem(me + i, seqs), shard),
            device_id_type=MESH,
        )

    def fact_arrival(i):
        return pltpu.make_async_remote_copy(
            src_ref=fact_ref,
            dst_ref=facts.at[lax.rem(me + seqs - i, seqs)],
            send_sem=f_s.at[i - 1],
            recv_sem=f_r.at[i - 1],
            device_id=(lax.rem(me + i, seqs), shard),
            device_id_type=MESH,
        )

    for i in range(1, seqs):
        fact_copy(i).start()
    place = lax.broadcasted_iota(jnp.int32, hot.shape, 0)
    hot[...] = jnp.where(place == flat_ref[...], 1.0, 0.0).astype(BF16)

    def pack_copy(n, i):
        return pltpu.make_async_copy(
            moved.at[n], packed[n].at[:, pl.ds(i * HG * d, HG * d)], pack_sem.at[n]
        )

    def group(i):
        for n, x_ref in enumerate((k_ref, v_ref, q_ref)):
            if i > 0:
                pack_copy(n, i - 1).wait()
            tall[...] = x_ref[:, i * HG : (i + 1) * HG, :].astype(F32).reshape(rows * HG, d)
            for j in range(HG):
                wide[:, j * d : (j + 1) * d] = tall[pl.ds(j, rows, stride=HG), :].astype(BF16)
            for j in range(HG // 2):
                cols = slice(2 * j * d, 2 * (j + 1) * d)
                rowsout = jnp.dot(hot[...], wide[:, cols], preferred_element_type=F32)
                moved[n, :, cols] = rowsout.astype(BF16)
            pack_copy(n, i).start()

        def body(g, _):
            here = pl.ds(pl.multiple_of(g * cap, 16), cap)
            weight = kw_ref[i, here, :]
            for j in range(HG):
                cols = slice(j * d, (j + 1) * d)
                scaled = (moved[0, here, cols].astype(F32) * weight[:, j : j + 1]).astype(BF16)
                update = lax.dot_general(
                    scaled,
                    moved[1, here, cols],
                    (((0,), (0,)), ((), ())),
                    preferred_element_type=F32,
                )
                u_ref[lax.div(g, 2), lax.rem(g, 2), i * HG + j] = update.astype(BF16)
            return 0

        lax.fori_loop(0, seqs, body, 0)
        for c in range(i * HG // HC, (i + 1) * HG // HC):
            up_copy(0, c).start()

    group(0)
    facts[pl.ds(me, 1)] = fact_ref[...][None]
    for i in range(1, seqs):
        fact_arrival(i).wait_recv()
    rate = rate_ref[...]
    spans = [((me // 2 ** (k + 1) * 2 + 1) * 2**k, 2**k) for k in range(levels)]
    spans += [((me // 2 ** (k + 1) * 2) * 2**k, 2**k) for k in range(levels)]
    spans += [(me * 0, seqs)]
    for table, (begin, size) in enumerate(spans):
        count = jnp.zeros(fact_ref.shape[1:], F32)
        docs = jnp.zeros(fact_ref.shape[1:], F32)
        for loader in range(seqs):
            inside = ((loader >= begin) & (loader < begin + size)).astype(F32)
            count = count + facts[loader, 0] * inside
            docs = docs + facts[loader, 1] * inside
        for seq in range(seqs):
            gone = jnp.exp(-rate * count[seq : seq + 1])
            dec[table * seqs + seq] = jnp.where(docs[seq : seq + 1] == 0.0, gone, 0.0)
    z_lag = levels - 1 + ZLAG
    per_group = HG // HC
    for t in range(chunks + z_lag + levels + 1):
        if t > 0 and t % per_group == 0 and t // per_group < heads // HG:
            group(t // per_group)
        for k in range(levels):
            if 0 <= t - k < chunks:
                up(k, t - k)
        if 0 <= t - z_lag < chunks:
            across(t - z_lag)
        for k in range(levels - 1, -1, -1):
            c = t - z_lag - (levels - 1 - k)
            if 0 <= c < chunks:
                down(k, c)
    for n in range(3):
        pack_copy(n, heads // HG - 1).wait()
    for c in range(chunks):
        for j in range(2 ** (levels - 1)):
            down_copy(0, c, j, True).wait_recv()
        for k in range(levels):
            up_copy(k, c).wait_send()
            for j in range(2 ** (levels - k - 1)):
                down_copy(k, c, j, False).wait_send()

    for i in range(1, seqs):
        fact_copy(i).wait_send()

    @pl.when(shard < shards - 1)
    def _():
        for c in range(chunks):
            z_copy(c, shard + 1).wait_send()


def scan_states(facts, rate, flat, key, value, query, key_weight, levels, shards, cap, call):
    rows, heads, d = key.shape
    seqs = facts.shape[1]
    total = seqs * cap
    chunks = heads // HC
    vm = pltpu.VMEM
    share = [2 ** (levels - k - 1) for k in range(levels)]
    dma = pltpu.SemaphoreType.DMA
    kw = key_weight.reshape(total, heads // HG, HG).transpose(1, 0, 2)
    packed_shape = jax.ShapeDtypeStruct((total, heads * d), BF16)
    return pl.pallas_call(
        functools.partial(scan_kernel, levels, shards, seqs, heads, cap),
        out_shape=[jax.ShapeDtypeStruct((seqs, heads, d, d), BF16)] + [packed_shape] * 3,
        in_specs=[pl.BlockSpec(memory_space=pltpu.VMEM)] * 7,
        out_specs=[pl.BlockSpec(memory_space=pltpu.VMEM)] + [pl.BlockSpec(memory_space=pl.ANY)] * 3,
        scratch_shapes=[
            vm((seqs // 2, 2, heads, d, d), BF16),
            vm((total, rows), BF16),
            vm((rows * HG, d), F32),
            vm((rows, HG * d), BF16),
            vm((3, total, HG * d), BF16),
            dma((3,)),
        ]
        + [vm((share[k], 2, heads, d, d), BF16) for k in range(1, levels)]
        + [vm((seqs,) + facts.shape, F32), vm(((2 * levels + 1) * seqs, heads, d), F32)]
        + [dma((seqs - 1,)), dma((seqs - 1,))]
        + [vm((share[k], heads, d, d), BF16) for k in range(levels)]
        + [vm((heads, d, d), ZT), vm((heads, d, d), ZT)]
        + [dma((levels, chunks)), dma((levels, chunks))]
        + [dma((seqs - 1, chunks)), dma((seqs - 1, chunks))]
        + [dma((chunks,)), dma((chunks,))],
        compiler_params=pltpu.CompilerParams(
            collective_id=call, has_side_effects=True, vmem_limit_bytes=67043328
        ),
    )(facts, rate, flat.reshape(1, rows), key, value, query, kw)


def finish_kernel(
    heads, d, rate_ref, flat_ref, q_ref, k_ref, v_ref, state_ref, col_ref, row_ref, cw_ref, gain_ref,
    o_ref, mixed, normed, tall
):
    cap = q_ref.shape[0]
    g = pl.program_id(0)
    ri = lax.broadcasted_iota(jnp.int32, (cap, cap), 0)
    ci = lax.broadcasted_iota(jnp.int32, (cap, cap), 1)
    keep = (ri >= ci) & (col_ref[...] == row_ref[0])
    gap = jnp.maximum(ri - ci, 0).astype(F32)
    carry = cw_ref[...]
    squares = jnp.zeros((cap, d), F32)
    for h in range(heads):
        cols = slice(h * d, (h + 1) * d)
        q = q_ref[:, cols]
        scores = lax.dot_general(
            q, k_ref[:, cols], (((1,), (1,)), ((), ())), preferred_element_type=F32
        )
        weight = jnp.where(keep, jnp.exp(-rate_ref[h] * gap), 0.0)
        half = (scores * weight).astype(BF16)
        intra = jnp.dot(half, v_ref[:, cols], preferred_element_type=F32)
        inter = jnp.dot(q, state_ref[0, h], preferred_element_type=F32)
        out = intra + inter * carry[:, h : h + 1]
        mixed[:, cols] = out
        squares = squares + out * out
    mean = jnp.sum(squares, axis=1, keepdims=True) * (1.0 / (heads * d))
    scale = lax.rsqrt(mean + eps_norm)
    for h in range(heads):
        cols = slice(h * d, (h + 1) * d)
        result = (mixed[:, cols] * scale * gain_ref[:, cols]).astype(BF16)
        normed[pl.ds(pl.multiple_of(g * cap, 16), cap), cols] = result

    @pl.when(g == pl.num_programs(0) - 1)
    def _():
        rows, total = o_ref.shape[0], normed.shape[0]
        place = lax.broadcasted_iota(jnp.int32, (rows, total), 1)
        hot = jnp.where(place == flat_ref[...], 1.0, 0.0).astype(BF16)
        for i in range(heads // HO):
            for j in range(0, HO, 2):
                h = i * HO + j
                back = jnp.dot(hot, normed[:, h * d : (h + 2) * d], preferred_element_type=F32)
                tall[pl.ds(j, rows, stride=HO), :] = back[:, :d]
                tall[pl.ds(j + 1, rows, stride=HO), :] = back[:, d:]
            o_ref[:, i * HO : (i + 1) * HO, :] = tall[...].reshape(rows, HO, d).astype(BF16)


def finish(rate, flat, query, key, value, states, doc, carry_weight, gain, seqs, cap, heads, d):
    total = seqs * cap
    rows = flat.shape[0]
    wide = pl.BlockSpec((cap, heads * d), lambda g: (g, 0))
    return pl.pallas_call(
        functools.partial(finish_kernel, heads, d),
        grid=(seqs,),
        out_shape=jax.ShapeDtypeStruct((rows, heads, d), BF16),
        in_specs=[
            pl.BlockSpec(memory_space=pltpu.SMEM),
            pl.BlockSpec((rows, 1), lambda g: (0, 0)),
            wide,
            wide,
            wide,
            pl.BlockSpec((1, heads, d, d), lambda g: (g, 0, 0, 0)),
            pl.BlockSpec((cap, 1), lambda g: (g, 0)),
            pl.BlockSpec((1, 1, cap), lambda g: (g, 0, 0)),
            pl.BlockSpec((cap, heads), lambda g: (g, 0)),
            pl.BlockSpec((1, heads * d), lambda g: (0, 0)),
        ],
        out_specs=pl.BlockSpec((rows, heads, d), lambda g: (0, 0, 0)),
        scratch_shapes=[
            pltpu.VMEM((cap, heads * d), F32),
            pltpu.VMEM((total, heads * d), BF16),
            pltpu.VMEM((rows * HO, d), F32),
        ],
        compiler_params=pltpu.CompilerParams(vmem_limit_bytes=56 * 1024 * 1024),
    )(
        rate,
        flat.reshape(rows, 1),
        query,
        key,
        value,
        states,
        doc.reshape(total, 1),
        doc.reshape(seqs, 1, cap),
        carry_weight,
        gain.reshape(1, heads * d),
    )


def per_device(queries, key_rows, value_rows, destination, doc_starts, decay_rate, norm_gain):
    loaders = lax.axis_size("dp")
    shards = lax.axis_size("seq")
    rows, heads, d = queries.shape[2:]
    cap = 3 * rows // (2 * loaders)
    levels = loaders.bit_length() - 1
    total = loaders * cap
    dest = destination[0, 0]
    start = doc_starts[0, 0]
    r = jnp.arange(rows, dtype=jnp.int32)
    earlier = (dest[:, None] == dest[None, :]) & (r[None, :] < r[:, None])
    slot = jnp.sum(earlier.astype(jnp.int32), axis=1)
    flat = dest * cap + slot
    place = jnp.arange(total, dtype=jnp.int32)
    hit = place[:, None] == flat[None, :]
    begin = jnp.sum(jnp.where(hit, start[None, :], 0), axis=1).reshape(loaders, cap)
    targets = jnp.arange(loaders, dtype=jnp.int32)
    number = jnp.sum((dest[None, :] == targets[:, None]).astype(jnp.int32), axis=1)
    position = jnp.arange(cap, dtype=jnp.int32)
    upto = (position[None, :] <= position[:, None]).astype(jnp.int32)
    doc = jnp.sum(begin[:, None, :] * upto[None], axis=2)
    doc_end = jnp.sum(begin, axis=1)

    facts = jnp.broadcast_to(jnp.stack([number, doc_end]).astype(F32)[:, :, None], (2, loaders, d))
    rate = jnp.broadcast_to(decay_rate[:, None], (heads, d))

    until = jnp.maximum(number[:, None] - 1 - position[None, :], 0).astype(F32)
    key_keep = (position[None, :] < number[:, None]) & (doc == doc_end[:, None])
    key_weight = jnp.where(
        key_keep[:, :, None], jnp.exp(-decay_rate[None, None, :] * until[:, :, None]), 0.0
    ).reshape(total, heads)
    since = (position + 1).astype(F32)
    carry_weight = jnp.where(
        (doc == 0)[:, :, None], jnp.exp(-decay_rate[None, None, :] * since[None, :, None]), 0.0
    ).reshape(total, heads)

    passes = max(1, loaders // 8)
    width = heads // passes
    results = []
    for i in range(passes):
        part = slice(i * width, (i + 1) * width)
        results.append(
            scan_states(
                facts,
                rate[part],
                flat,
                key_rows[0, 0, :, part],
                value_rows[0, 0, :, part],
                queries[0, 0, :, part],
                key_weight[:, part],
                levels,
                shards,
                cap,
                i,
            )
        )
    states, key, value, query = [
        x[0] if passes == 1 else jnp.concatenate(x, axis=1) for x in zip(*results)
    ]
    attended = finish(
        decay_rate, flat, query, key, value, states, doc, carry_weight, norm_gain, loaders, cap, heads, d
    )
    return attended[None, None]


def solution(mesh):
    placed = (
        P("dp", "seq", None, None, None),
        P("dp", "seq", None, None, None),
        P("dp", "seq", None, None, None),
        P("dp", "seq", None),
        P("dp", "seq", None),
        P(),
        P(),
    )
    return jax.shard_map(
        per_device,
        mesh=mesh,
        in_specs=placed,
        out_specs=P("dp", "seq", None, None, None),
        check_vma=False,
    )
```
